32 devices in a mesh: replica: 2 (over core), shard: 16 (over z, y, x).
Axes of the slice: x: 2, y: 2, z: 4, core: 2. Of those that a mesh axis runs over, the one named last changes fastest.
Arguments:
- gradients: bfloat16 [2, 2, 16, 1024, 256], P('replica', None, None, 'shard'), may hold values from -36 to 36
- momentum: float32 [2, 16, 1024, 256], P('replica', None, 'shard'), may hold values from -3 to 3
- params: float32 [16, 1024, 256], P(None, ('shard', 'replica')), may hold values from -6 to 6
- outer_moment: float32 [16, 1024, 256], P(None, ('shard', 'replica')), may hold values from -2 to 2
- shadow: float32 [16, 1024, 256], P(None, ('shard', 'replica')), may hold values from -6 to 6
Outputs:
- new_params: float32 [16, 1024, 256], P(None, ('shard', 'replica'))
- new_outer_moment: float32 [16, 1024, 256], P(None, ('shard', 'replica'))
- new_shadow: float32 [16, 1024, 256], P(None, ('shard', 'replica'))
- new_momentum: float32 [2, 16, 1024, 256], P('replica', None, 'shard')
The draws below stay inside these ranges and needn't reach their ends.
All inputs are finite; a program needn't handle non-finite values.
Results may differ from the reference program's by a relative error of at most 0.0085.
Values may be sent and summed in bfloat16 or wider, within the bound.
No kernel may reach another device: no remote copies, remote signals or barrier semaphores. Data moves between devices by JAX's collectives and lax.ppermute only.
A program may use at most 64 MiB of HBM per device.

```python
import math
import jax
import jax.numpy as jnp
from jax import lax

D = 1024
FF = 256
INNER = 2
NS_ITERS = 5
MATS = 16
N_REPLICA = 2


def draw_gradients(key, part):
    shape = (N_REPLICA, INNER, MATS, D, FF)
    key_base, key_rows, key_cols = jax.random.split(key, 3)
    row_scale = jnp.exp(jax.random.uniform(key_rows, (N_REPLICA, INNER, MATS, D, 1), jnp.float32, math.log(0.3), math.log(3.0)))
    col_scale = jnp.exp(jax.random.uniform(key_cols, (N_REPLICA, INNER, MATS, 1, FF), jnp.float32, math.log(0.3), math.log(3.0)))
    base = jnp.clip(jax.random.normal(key_base, shape, jnp.float32), -4.0, 4.0)
    return (base * row_scale * col_scale).astype(jnp.bfloat16)


def block_scale(key, dims, pieces, least, top_value):
    def one(dim, parts):
        draws = jax.random.uniform(jax.random.fold_in(jax.random.fold_in(key, 6), dim), (parts,), jnp.float32, least / len(pieces), top_value / len(pieces))
        return jnp.repeat(jnp.exp(draws), dims[dim] // parts).reshape((-1,) + (1,) * (len(dims) - dim - 1))

    gain = one(*pieces[0])
    for cut in pieces[1:]:
        gain = gain * one(*cut)
    return gain


def bell_draw(own_key, shape, width, limit, pieces=(), kind=jnp.bfloat16):
    level = block_scale(own_key, shape, pieces, -0.22, 0.18) if pieces else 1.0
    array = jax.random.normal(own_key, shape, jnp.float32) * width * level
    return jnp.minimum(jnp.maximum(array, -limit), limit).astype(kind)


def setup_inputs(seed: int = 0) -> dict:
    key_list = jax.random.split(jax.random.key(seed), 6)
    gradients = draw_gradients(jax.random.fold_in(key_list[5], 71), 0)
    momentum = bell_draw(key_list[1], (N_REPLICA, MATS, D, FF), 0.5, 3.0, ((0, 2), (2, 16)), jnp.float32)
    params = bell_draw(key_list[2], (MATS, D, FF), 1.0, 6.0, ((1, 32),), jnp.float32)
    outer_moment = bell_draw(key_list[3], (MATS, D, FF), 0.3, 2.0, ((1, 32),), jnp.float32)
    shadow = bell_draw(key_list[4], (MATS, D, FF), 1.0, 6.0, ((1, 32),), jnp.float32)
    return {"gradients": gradients, "momentum": momentum, "params": params, "outer_moment": outer_moment, "shadow": shadow}


quintic_a = 3.4445
quintic_b = -4.775
quintic_c = 2.0315
inner_beta = 0.95
outer_mu = 0.9
outer_rate = 0.7
shadow_decay = 0.9

def orthogonalize(update):
    squares = jnp.sum(jnp.square(update.astype(jnp.float32)))
    current = (update.astype(jnp.float32) / (jnp.sqrt(squares) + 1e-07)).astype(jnp.bfloat16)
    for repeat in range(NS_ITERS):
        gram_block = jnp.dot(current.T, current, preferred_element_type=jnp.float32).astype(jnp.bfloat16)
        square = jnp.dot(gram_block, gram_block, preferred_element_type=jnp.float32)
        polynomial = (quintic_b * gram_block.astype(jnp.float32) + quintic_c * square).astype(jnp.bfloat16)
        product = jnp.dot(current, polynomial, preferred_element_type=jnp.float32)
        current = (quintic_a * current.astype(jnp.float32) + product).astype(jnp.bfloat16)
    return current

def reference(gradients, momentum, params, outer_moment, shadow):
    scale_step = 0.2 * math.sqrt(D)
    deltas = jnp.zeros(params.shape, jnp.float32)
    moments = []
    for replica in range(N_REPLICA):
        moment_now = momentum[replica]
        total = jnp.zeros(params.shape, jnp.float32)
        for position in range(INNER):
            grad_now = gradients[replica, position].astype(jnp.float32)
            moment_now = inner_beta * moment_now + grad_now
            update = (grad_now + inner_beta * moment_now).astype(jnp.bfloat16)
            orthos = lax.map(orthogonalize, update)
            total = total + scale_step * orthos.astype(jnp.float32)
        deltas = deltas + total
        moments.append(moment_now)
    outer_delta = deltas / N_REPLICA
    new_outer = outer_mu * outer_moment + outer_delta
    new_params = params - outer_rate * (outer_delta + outer_mu * new_outer)
    new_shadow = shadow_decay * shadow + (1.0 - shadow_decay) * new_params
    return (new_params, new_outer, new_shadow, jnp.stack(moments))
```

```python
import math

import jax
import jax.numpy as jnp
from jax import lax
from jax.sharding import PartitionSpec as P

NS_ITERS = 5

quintic_a = 3.4445
quintic_b = -4.775
quintic_c = 2.0315
inner_beta = 0.95
outer_mu = 0.9
outer_rate = 0.7
shadow_decay = 0.9


def newton_schulz(block):
    squares = jnp.sum(jnp.square(block.astype(jnp.float32)))
    current = (block.astype(jnp.float32) / (jnp.sqrt(squares) + 1e-07)).astype(jnp.bfloat16)
    for _ in range(NS_ITERS):
        gram = jnp.einsum(
            "di,dj->ij", current, current, preferred_element_type=jnp.float32
        ).astype(jnp.bfloat16)
        square = jnp.dot(gram, gram, preferred_element_type=jnp.float32)
        poly = (quintic_b * gram.astype(jnp.float32) + quintic_c * square).astype(jnp.bfloat16)
        product = jnp.dot(current, poly, preferred_element_type=jnp.float32)
        current = (quintic_a * current.astype(jnp.float32) + product).astype(jnp.bfloat16)
    return current


def body(gradients, momentum, params, outer_moment, shadow):
    shards = lax.axis_size("shard")
    replicas = lax.axis_size("replica")
    _, inner, mats, rows, width = gradients.shape
    owned = mats // shards
    total_rows = rows * shards
    rows_each = rows // replicas
    scale_step = 0.2 * math.sqrt(total_rows)

    moment = momentum[0]
    updates = []
    for k in range(inner):
        grad = gradients[0, k].astype(jnp.float32)
        moment = inner_beta * moment + grad
        updates.append((grad + inner_beta * moment).astype(jnp.bfloat16))
    stacked = jnp.stack(updates, axis=1)
    moved = lax.all_to_all(stacked, "shard", split_axis=0, concat_axis=0, tiled=True)
    moved = moved.reshape((shards, owned, inner, rows, width))

    totals = []
    for m in range(owned):
        total = None
        for k in range(inner):
            ortho = newton_schulz(moved[:, m, k].reshape((total_rows, width)))
            term = scale_step * ortho.astype(jnp.float32)
            total = term if total is None else total + term
        totals.append(total)
    total = jnp.stack(totals).reshape((owned, shards, replicas, rows_each, width))

    me = lax.axis_index("replica")
    summed = lax.dynamic_index_in_dim(total, me, 2, keepdims=False)
    for step in range(1, replicas):
        theirs = lax.dynamic_index_in_dim(total, (me + step) % replicas, 2, keepdims=False)
        got = lax.ppermute(
            theirs.astype(jnp.bfloat16),
            "replica",
            [(i, (i + step) % replicas) for i in range(replicas)],
        )
        summed = summed + got.astype(jnp.float32)
    placed = lax.all_to_all(
        summed.astype(jnp.bfloat16), "shard", split_axis=1, concat_axis=0, tiled=True
    )
    outer_delta = placed.reshape((mats, rows_each, width)).astype(jnp.float32) / replicas
    new_outer = outer_mu * outer_moment + outer_delta
    new_params = params - outer_rate * (outer_delta + outer_mu * new_outer)
    new_shadow = shadow_decay * shadow + (1.0 - shadow_decay) * new_params
    return (new_params, new_outer, new_shadow, moment[None])


def solution(mesh):
    rows = P(None, ("shard", "replica"), None)
    mine = P("replica", None, "shard", None)
    return jax.shard_map(
        body,
        mesh=mesh,
        in_specs=(P("replica", None, None, "shard", None), mine, rows, rows, rows),
        out_specs=(rows, rows, rows, mine),
        check_vma=False,
    )
```

```python
import functools
import math

import jax
import jax.numpy as jnp
from jax import lax
from jax.experimental import pallas as pl
from jax.experimental.pallas import tpu as pltpu
from jax.sharding import PartitionSpec as P

NS_ITERS = 5

quintic_a = 3.4445
quintic_b = -4.775
quintic_c = 2.0315
inner_beta = 0.95
outer_mu = 0.9
outer_rate = 0.7
shadow_decay = 0.9

f32 = jnp.float32
bf16 = jnp.bfloat16
VMEM = pl.BlockSpec(memory_space=pltpu.VMEM)
SMEM = pl.BlockSpec(memory_space=pltpu.SMEM)


def gram_of(x):
    return lax.dot_general(x, x, (((0,), (0,)), ((), ())), preferred_element_type=f32)


def poly_of(gram):
    gram = gram.astype(bf16)
    square = jnp.dot(gram, gram, preferred_element_type=f32)
    return (quintic_b * gram.astype(f32) + quintic_c * square).astype(bf16)


def step_of(x, poly):
    return quintic_a * x.astype(f32) + jnp.dot(x, poly, preferred_element_type=f32)


def ns_kernel(me_ref, moved_ref, *refs, replicas):
    shards, inner, rows, width = moved_ref.shape
    outs, total_ref = refs[:replicas], refs[replicas]
    n_rows = shards * rows
    xs = [moved_ref[:, k].reshape(n_rows, width) for k in range(inner)]
    row = lax.broadcasted_iota(jnp.int32, (width, width), 0)
    diagonal = row == lax.broadcasted_iota(jnp.int32, (width, width), 1)
    grams = [gram_of(x) for x in xs]
    scales = []
    for gram in grams:
        squares = jnp.full((1, 1), jnp.sum(jnp.where(diagonal, gram, 0.0)), f32)
        scales.append(1.0 / (jnp.sqrt(squares) + 1e-07))
    polys = [poly_of(g * (s * s)) for g, s in zip(grams, scales)]
    xs = [(step_of(x, p) * s).astype(bf16) for x, p, s in zip(xs, polys, scales)]
    for _ in range(NS_ITERS - 2):
        polys = [poly_of(gram_of(x)) for x in xs]
        xs = [step_of(x, p).astype(bf16) for x, p in zip(xs, polys)]
    polys = [poly_of(gram_of(x)) for x in xs]
    total = None
    for x, p in zip(xs, polys):
        ortho = step_of(x, p)
        total = ortho if total is None else total + ortho
    total = (0.2 * math.sqrt(n_rows)) * total
    total_ref[...] = total.astype(bf16).reshape(total_ref.shape)
    me = me_ref[0]
    for s in range(shards):
        for d in range(replicas):
            outs[d][s] = total_ref[s * replicas + lax.rem(me + d, replicas)]


def orthogonal_parts(me, moved, replicas):
    shards, inner, rows, width = moved.shape
    rows_each = rows // replicas
    part = jax.ShapeDtypeStruct((shards, rows_each, width), bf16)
    return pl.pallas_call(
        functools.partial(ns_kernel, replicas=replicas),
        out_shape=[part] * replicas,
        in_specs=[SMEM, VMEM],
        out_specs=[VMEM] * replicas,
        scratch_shapes=[pltpu.VMEM((shards * replicas, rows_each, width), bf16)],
        compiler_params=pltpu.CompilerParams(vmem_limit_bytes=32 * 1024 * 1024),
        name="newton_schulz",
    )(me, moved)


def body(gradients, momentum, params, outer_moment, shadow):
    shards = lax.axis_size("shard")
    replicas = lax.axis_size("replica")
    _, inner, mats, rows, width = gradients.shape
    owned = mats // shards
    rows_each = rows // replicas

    moment = momentum[0]
    updates = []
    for k in range(inner):
        grad = gradients[0, k].astype(f32)
        moment = inner_beta * moment + grad
        updates.append((grad + inner_beta * moment).astype(bf16))
    stacked = jnp.stack(updates, axis=1)
    moved = lax.all_to_all(stacked, "shard", split_axis=0, concat_axis=0, tiled=True)
    moved = moved.reshape((shards, owned, inner, rows, width))

    me = lax.axis_index("replica").astype(jnp.int32)[None]
    summed = []
    for m in range(owned):
        parts = orthogonal_parts(me, moved[:, m], replicas)
        part = parts[0].astype(f32)
        for step in range(1, replicas):
            pairs = [(i, (i + step) % replicas) for i in range(replicas)]
            part = part + lax.ppermute(parts[step], "replica", pairs).astype(f32)
        summed.append(part.astype(bf16))
    summed = jnp.stack(summed)
    placed = lax.all_to_all(summed, "shard", split_axis=1, concat_axis=0, tiled=True)
    outer_delta = placed.reshape((mats, rows_each, width)).astype(f32) / replicas
    new_outer = outer_mu * outer_moment + outer_delta
    new_params = params - outer_rate * (outer_delta + outer_mu * new_outer)
    new_shadow = shadow_decay * shadow + (1.0 - shadow_decay) * new_params
    return (new_params, new_outer, new_shadow, moment[None])


def solution(mesh):
    rows = P(None, ("shard", "replica"), None)
    mine = P("replica", None, "shard", None)
    return jax.shard_map(
        body,
        mesh=mesh,
        in_specs=(P("replica", None, None, "shard", None), mine, rows, rows, rows),
        out_specs=(rows, rows, rows, mine),
        check_vma=False,
    )
```

```python
import functools
import math

import jax
import jax.numpy as jnp
from jax import lax
from jax.experimental import pallas as pl
from jax.experimental.pallas import tpu as pltpu
from jax.sharding import PartitionSpec as P

NS_ITERS = 5

quintic_a = 3.4445
quintic_b = -4.775
quintic_c = 2.0315
inner_beta = 0.95
outer_mu = 0.9
outer_rate = 0.7
shadow_decay = 0.9


f32 = jnp.float32
bf16 = jnp.bfloat16
VMEM = pl.BlockSpec(memory_space=pltpu.VMEM)
SMEM = pl.BlockSpec(memory_space=pltpu.SMEM)
ANY = pl.BlockSpec(memory_space=pl.ANY)


def grid_of(shards):
    lo = max(n for n in range(1, math.isqrt(shards) + 1) if shards % n == 0)
    return shards // lo, lo


def is_power(n):
    return n & (n - 1) == 0


def to_of(i, d, n):
    return i ^ d if is_power(n) else lax.rem(i + d, n)


def from_of(i, d, n):
    return i ^ d if is_power(n) else lax.rem(i + n - d, n)


def far_pairs(d, hi, lo):
    return [(z * lo + c, int(to_of(z, d, hi)) * lo + c) for z in range(hi) for c in range(lo)]


def near_pairs(j, hi, lo):
    return [(z * lo + c, z * lo + int(to_of(c, j, lo))) for z in range(hi) for c in range(lo)]


def update_kernel(where_ref, grad_ref, moment_ref, *refs, hi, lo, owned):
    outs, (grads, moments, sems) = refs[:hi], refs[hi:]
    z, c = where_ref[0], where_ref[1]
    order = list(range(hi - 1, -1, -1))
    copies = {}
    for d in order:
        block = pl.ds(to_of(z, d, hi) * lo, lo)
        copies[d] = (
            pltpu.make_async_copy(grad_ref.at[block], grads.at[d], sems.at[0, d]),
            pltpu.make_async_copy(moment_ref.at[block], moments.at[d], sems.at[1, d]),
        )
        for copy in copies[d]:
            copy.start()
    for d in order:
        for copy in copies[d]:
            copy.wait()
        for j in range(lo):
            near = to_of(c, j, lo)
            grad = grads[d, near].astype(f32)
            moment = inner_beta * moments[d, near] + grad
            outs[d][j] = (grad + inner_beta * moment).astype(bf16)


def first_update(where, grad, moment, hi, lo):
    mats, rows, width = grad.shape
    owned = mats // (hi * lo)
    view = (hi * lo, owned, rows, width)
    block = (lo, owned, rows, width)
    return pl.pallas_call(
        functools.partial(update_kernel, hi=hi, lo=lo, owned=owned),
        out_shape=[jax.ShapeDtypeStruct(block, bf16)] * hi,
        in_specs=[SMEM, ANY, ANY],
        out_specs=[VMEM] * hi,
        scratch_shapes=[
            pltpu.VMEM((hi,) + block, bf16),
            pltpu.VMEM((hi,) + block, f32),
            pltpu.SemaphoreType.DMA((2, hi)),
        ],
        compiler_params=pltpu.CompilerParams(vmem_limit_bytes=16 * 1024 * 1024),
        name="first_update",
    )(where, grad.reshape(view), moment.reshape(view))


def gram_of(y):
    return lax.dot_general(y, y, (((1,), (1,)), ((), ())), preferred_element_type=f32)


def poly_of(gram):
    gram = gram.astype(bf16)
    square = jnp.dot(gram, gram, preferred_element_type=f32)
    return (quintic_b * gram.astype(f32) + quintic_c * square).astype(bf16)


def step_of(y, poly):
    return quintic_a * y.astype(f32) + jnp.dot(poly, y, preferred_element_type=f32)


def chain_of(y, diagonal):
    gram = gram_of(y)
    yield None
    squares = jnp.full((1, 1), jnp.sum(jnp.where(diagonal, gram, 0.0)), f32)
    scale = 1.0 / (jnp.sqrt(squares) + 1e-07)
    poly = poly_of(gram * (scale * scale))
    yield None
    y = (step_of(y, poly) * scale).astype(bf16)
    yield None
    for left in range(NS_ITERS - 2, -1, -1):
        gram = gram_of(y)
        yield None
        poly = poly_of(gram)
        yield None
        y = step_of(y, poly)
        if left:
            y = y.astype(bf16)
        yield None if left else y


def staggered(chains):
    results = [None] * len(chains)
    live = set(range(len(chains)))
    tick = 0
    while live:
        for k in sorted(live):
            if tick >= k:
                try:
                    results[k] = next(chains[k])
                except StopIteration:
                    live.discard(k)
        tick += 1
    return results


def ns_kernel(where_ref, *refs, hi, lo, replicas):
    far, near = refs[:hi], refs[hi : hi + lo - 1]
    rest_ref = refs[hi + lo - 1]
    outs = refs[hi + lo : hi + lo + replicas]
    first_ref, total_ref = refs[hi + lo + replicas :]
    shards, rest, rows, width = rest_ref.shape
    n_rows = shards * rows
    z, c, me = where_ref[0], where_ref[1], where_ref[2]
    for d in range(hi):
        at = from_of(z, d, hi) * lo
        first_ref[at + c] = far[d][...]
        for j in range(1, lo):
            first_ref[at + from_of(c, j, lo)] = near[j - 1][d]
    xs = [first_ref[...]] + [rest_ref[:, k] for k in range(rest)]
    ys = [x.reshape(n_rows, width).T for x in xs]
    row = lax.broadcasted_iota(jnp.int32, (width, width), 0)
    diagonal = row == lax.broadcasted_iota(jnp.int32, (width, width), 1)
    orthos = staggered([chain_of(y, diagonal) for y in ys])
    total = orthos[0]
    for ortho in orthos[1:]:
        total = total + ortho
    total = ((0.2 * math.sqrt(n_rows)) * total).astype(bf16)
    total_ref[...] = total.T.reshape(total_ref.shape)
    for s in range(shards):
        for d in range(replicas):
            outs[d][s] = total_ref[s * replicas + lax.rem(me + d, replicas)]


def orthogonal_parts(where, far, near, rest, hi, lo, replicas):
    shards, _, rows, width = rest.shape
    rows_each = rows // replicas
    part = jax.ShapeDtypeStruct((shards, rows_each, width), bf16)
    return pl.pallas_call(
        functools.partial(ns_kernel, hi=hi, lo=lo, replicas=replicas),
        out_shape=[part] * replicas,
        in_specs=[SMEM] + [VMEM] * (hi + lo),
        out_specs=[VMEM] * replicas,
        scratch_shapes=[
            pltpu.VMEM((shards, rows, width), bf16),
            pltpu.VMEM((shards * replicas, rows_each, width), bf16),
        ],
        compiler_params=pltpu.CompilerParams(vmem_limit_bytes=32 * 1024 * 1024),
        name="newton_schulz",
    )(where, *far, *near, rest)


def body(gradients, momentum, params, outer_moment, shadow):
    shards = lax.axis_size("shard")
    replicas = lax.axis_size("replica")
    _, inner, mats, rows, width = gradients.shape
    owned = mats // shards
    rows_each = rows // replicas
    hi, lo = grid_of(shards)
    shard = lax.axis_index("shard")
    where = jnp.stack([shard // lo, shard % lo, lax.axis_index("replica")]).astype(jnp.int32)

    blocks = first_update(where, gradients[0, 0], momentum[0], hi, lo)
    far = [blocks[0]] + [None] * (hi - 1)
    for d in range(hi - 1, 0, -1):
        far[d] = lax.ppermute(blocks[d], "shard", far_pairs(d, hi, lo))

    moment = momentum[0]
    updates = []
    for k in range(inner):
        grad = gradients[0, k].astype(f32)
        moment = inner_beta * moment + grad
        updates.append((grad + inner_beta * moment).astype(bf16))
    rest = jnp.stack(updates[1:], axis=1)
    rest = lax.all_to_all(rest, "shard", split_axis=0, concat_axis=0, tiled=True)
    rest = rest.reshape((shards, owned, inner - 1, rows, width))

    near = []
    for j in range(1, lo):
        passed = jnp.stack([block[j] for block in far])
        near.append(lax.ppermute(passed, "shard", near_pairs(j, hi, lo)))

    summed = []
    for m in range(owned):
        parts = orthogonal_parts(
            where,
            [block[0, m] for block in far],
            [block[:, m] for block in near],
            rest[:, m],
            hi,
            lo,
            replicas,
        )
        part = parts[0].astype(f32)
        for step in range(1, replicas):
            pairs = [(i, (i + step) % replicas) for i in range(replicas)]
            part = part + lax.ppermute(parts[step], "replica", pairs).astype(f32)
        summed.append(part.astype(bf16))
    summed = jnp.stack(summed)
    placed = lax.all_to_all(summed, "shard", split_axis=1, concat_axis=0, tiled=True)
    outer_delta = placed.reshape((mats, rows_each, width)).astype(f32) / replicas
    new_outer = outer_mu * outer_moment + outer_delta
    new_params = params - outer_rate * (outer_delta + outer_mu * new_outer)
    new_shadow = shadow_decay * shadow + (1.0 - shadow_decay) * new_params
    return (new_params, new_outer, new_shadow, moment[None])


def solution(mesh):
    rows = P(None, ("shard", "replica"), None)
    mine = P("replica", None, "shard", None)
    return jax.shard_map(
        body,
        mesh=mesh,
        in_specs=(P("replica", None, None, "shard", None), mine, rows, rows, rows),
        out_specs=(rows, rows, rows, mine),
        check_vma=False,
    )
```
